128 devices in a mesh: req: 16 (over x, z), ep: 8 (over y, core).
Axes of the slice: x: 4, y: 4, z: 4, core: 2. Of those that a mesh axis runs over, the one named last changes fastest.
Arguments:
- hidden: bfloat16 [16384, 1536], P(('req', 'ep')), may hold values from -6 to 6
- parents: int32 [256, 64], P(('req', 'ep')), may hold values from 0 to 62, as said below
- path: int32 [256, 64], P(('req', 'ep')), may hold values from -1 to 63, as said below
- cache_len: int32 [256], P(('req', 'ep')), may hold values from 64 to 1024
- page_table: int32 [256, 8], P(('req', 'ep')), may hold values from 0 to 15, as said below
- kv_pool: bfloat16 [2048, 128, 512], P(('req', 'ep')), may hold values from -90 to 90
- mig_slot: int32 [128], P(('req', 'ep')), may hold values from 0 to 1
- mig_dest: int32 [128], P(('req', 'ep')), may hold values from 0 to 7, as said below
- attn_gain: bfloat16 [1536], replicated, may hold values from 0.25 to 1.75
- w_qkv: bfloat16 [1536, 2048], replicated, may hold values from -0.15625 to 0.15625
- w_out: bfloat16 [1536, 1536], replicated, may hold values from -0.15625 to 0.15625
- moe_gain: bfloat16 [1536], replicated, may hold values from 0.25 to 1.75
- w_router: bfloat16 [1536, 32], replicated, may hold values from -0.15625 to 0.15625
- expert_ids: int32 [16384, 4], P(('req', 'ep')), may hold values from 0 to 31, all different within a row; in each aligned block of 128 rows (0 to 127, 128 to 255, ...) at most 32 rows name the same one
- w_gate: bfloat16 [128, 1536, 192], P(('req', 'ep')), may hold values from -0.15625 to 0.15625
- w_up: bfloat16 [128, 1536, 192], P(('req', 'ep')), may hold values from -0.15625 to 0.15625
- w_down: bfloat16 [128, 192, 1536], P(('req', 'ep')), may hold values from -0.21875 to 0.21875
Outputs:
- layer_out: bfloat16 [16384, 1536], P(('req', 'ep'))
- compact_kv: bfloat16 [256, 64, 512], P(('req', 'ep'))
The draws below stay inside these ranges and needn't reach their ends.
Inputs may be any that keep to these rules, and one draw needn't show every extreme that they name: parents[r, 0] = 0 marks the root; for i >= 1, parents[r, i] < i. `path`: row r lists a chain of the tree of parents[r] from the root 0 down to some token, each entry the parent of the next, then -1. `page_table`: the 2 requests of one device name each of its 16 pool pages once. `mig_dest`: within each index of req, the entries of its 8 devices form a permutation. `expert_ids`: each row names 4 different experts; among the rows of one device no expert is named by more than 32 rows.
All inputs are finite; a program needn't handle non-finite values.
Results may differ from the reference program's by a relative error of at most 0.015.
Values may be sent and summed in bfloat16 or wider, within the bound.
A program may use at most 128 MiB of HBM per device.

```python
import math
import jax
import jax.numpy as jnp
import numpy as np
from jax import lax

D = 1536
QUERY_HEADS = 12
KEY_VALUE_HEADS = 2
HEAD_SIZE = 128
EXPERTS = 32
FF = 768
TOPK = 4
DRAFT_TOKENS = 64
PAGE = 128
CONTEXT_LIMIT = 1024
R_DEV = 2
QKVW = 2048
KVW = 512
PAGES_REQ = 8
POOL = 16
REQUEST_COUNT = 256
TOK_DEV = 128
TOKENS = 16384
SPLIT = 4
FFS = 192
CAP = 32
N_REQ = 16
N_EP = 8
DEVICES = 128


def tree_parents(key):
    base = jax.random.fold_in(key, 11)
    steps = jnp.arange(DRAFT_TOKENS, dtype=jnp.int32)
    spread_pick = jax.random.randint(jax.random.fold_in(base, 1), (REQUEST_COUNT, DRAFT_TOKENS), 0, jnp.maximum(steps, 1)[None, :])
    coin_flip = jax.random.randint(jax.random.fold_in(base, 2), (REQUEST_COUNT, DRAFT_TOKENS), 0, 2)
    chained = jnp.maximum(steps - 1, 0)[None, :]
    parents = jnp.where(coin_flip == 1, chained, spread_pick).astype(jnp.int32)
    return parents.at[0, DRAFT_TOKENS - 1].set(DRAFT_TOKENS - 2)


def draw_parents(key, part):
    return tree_parents(key)


def draw_path(key, part):
    parents = tree_parents(key)
    backward = jax.random.randint(jax.random.fold_in(key, 23), (REQUEST_COUNT,), 0, max(1, DRAFT_TOKENS // 4))
    leaves = (DRAFT_TOKENS - 1 - backward).astype(jnp.int32).at[0].set(DRAFT_TOKENS - 1)

    def walk(parent_row, leaf_node):

        def stepper(current, unused_item):
            return (parent_row[current], current)
        unused_last, trail = lax.scan(stepper, leaf_node, None, length=DRAFT_TOKENS)
        depth_count = jnp.sum((trail != 0).astype(jnp.int32))
        columns = jnp.arange(DRAFT_TOKENS, dtype=jnp.int32)
        lookup = jnp.clip(depth_count - columns, 0, DRAFT_TOKENS - 1)
        return jnp.where(columns <= depth_count, trail[lookup], -1).astype(jnp.int32)
    return jax.vmap(walk)(parents, leaves)


def draw_cache_len(key, part):
    drawn = jax.random.randint(jax.random.fold_in(key, 5), (REQUEST_COUNT,), CONTEXT_LIMIT // 16, CONTEXT_LIMIT + 1).astype(jnp.int32)
    return drawn.at[0].set(CONTEXT_LIMIT).at[1].set(CONTEXT_LIMIT // 16)


def draw_page_table(key, part):

    def one_device(index):
        return jax.random.permutation(jax.random.fold_in(key, index + 31), POOL).astype(jnp.int32)
    tables = jax.vmap(one_device)(jnp.arange(N_REQ * N_EP, dtype=jnp.int32))
    return tables.reshape(REQUEST_COUNT, PAGES_REQ)


def draw_mig_dest(key, part):

    def one_group(index):
        return jax.random.permutation(jax.random.fold_in(key, index + 7), N_EP).astype(jnp.int32)
    return jax.vmap(one_group)(jnp.arange(N_REQ, dtype=jnp.int32)).reshape(N_REQ * N_EP)


def draw_kv_pool(key, part):
    shape_all = (N_REQ * N_EP * POOL, PAGE, KVW)
    first_key = jax.random.fold_in(key, 41)
    return jnp.clip(jax.random.normal(first_key, shape_all, jnp.float32), -6.0, 6.0).astype(jnp.bfloat16)


def set_ends(values, rng, smallest, top_value):
    place = [jax.random.randint(jax.random.fold_in(rng, axis), (), 0, length) for axis, length in enumerate(values.shape)]
    longest = values.shape.index(max(values.shape))
    neighbour = place[:longest] + [(place[longest] + 1) % values.shape[longest]] + place[longest + 1:]
    return values.at[tuple(place)].set(smallest).at[tuple(neighbour)].set(top_value)


def level_of(own_key, extent, cuts, low, high):
    def one(axis_at, parts):
        draws = jax.random.uniform(jax.random.fold_in(jax.random.fold_in(own_key, 6), axis_at), (parts,), jnp.float32, low / len(cuts), high / len(cuts))
        return jnp.repeat(jnp.exp(draws), extent[axis_at] // parts).reshape((-1,) + (1,) * (len(extent) - axis_at - 1))

    loudness = one(*cuts[0])
    for cut in cuts[1:]:
        loudness = loudness * one(*cut)
    return loudness


def deal_out(rng, own, number, rows, number_of, top, bound, skew):
    order = jax.random.permutation(rng, number_of)
    packed, usual = portions_of(number_of, rows * top, bound, skew, True), portions_of(number_of, rows * top, bound, skew, False)
    places = jnp.arange(number_of)

    def named(sizes, turn):
        used = int((sizes > 0).sum())
        fixed = max(1, used // 4)
        moved = fixed + (places - fixed + turn * (used - fixed)) % max(1, number_of - fixed)
        return jnp.zeros((number_of,), jnp.int32).at[order[jnp.where(places < fixed, places, moved)]].set(jnp.asarray(sizes, jnp.int32))

    sizes = jnp.where(number % 4 == 0, named(packed, number // 4), named(usual, number - number // 4 - 1))
    mixed = jax.random.permutation(jax.random.fold_in(own, 3), number_of)
    donor, receiver = mixed[0:number_of // 2 * 2:2], mixed[1:number_of // 2 * 2:2]
    room = jnp.minimum(sizes[donor] - 1, bound - sizes[receiver]) // 2
    room = jnp.where((donor == order[0]) | (receiver == order[0]) | (sizes[receiver] == 0), 0, jnp.maximum(room, 0))
    moved = jax.random.randint(jax.random.fold_in(own, 4), (number_of // 2,), 0, 1 << 20) % (room + 1)
    sizes = sizes.at[donor].add(-moved).at[receiver].add(moved)
    members = jnp.searchsorted(jnp.cumsum(sizes), jnp.arange(rows * top), side="right").astype(jnp.int32)
    table = members.reshape(top, rows).T
    table = table[jax.random.permutation(jax.random.fold_in(own, 1), rows)]
    turn = jax.random.randint(jax.random.fold_in(own, 2), (rows, 1), 0, top)
    return jnp.take_along_axis(table, (jnp.arange(top)[None, :] + turn) % top, axis=1)


def portions_of(number_of, total, bound, slope, full):
    loads = [(1 << 20) // math.isqrt(grade ** slope) + 1 for grade in range(1, number_of + 1)]
    largest = bound if full else min(bound, max(-(-total // number_of), total * loads[0] // sum(loads)))
    least = 1 if total - largest >= number_of - 1 else 0
    holding, spare = [largest] + [least] * (number_of - 1), total - largest - least * (number_of - 1)
    while spare > 0:
        free = [i for i in range(1, number_of) if holding[i] < largest] or [i for i in range(1, number_of) if holding[i] < bound]
        whole, left = sum([loads[i] for i in free]), spare
        for i in free:
            more = min(bound - holding[i], max(1, left * loads[i] // whole), spare)
            holding[i] = holding[i] + more
            spare = spare - more
    return np.array(holding)


def gaussian(stream_key, shape, width, bound, split=(), held_as=jnp.bfloat16):
    gain = level_of(stream_key, shape, split, -0.22, 0.18) if split else 1.0
    values = jax.random.normal(stream_key, shape, jnp.float32) * width * gain
    return jnp.minimum(jnp.maximum(values, -bound), bound).astype(held_as)


def setup_inputs(seed: int = 0) -> dict:
    key_of = jax.random.split(jax.random.key(seed), 18)
    hidden = gaussian(key_of[0], (TOKENS, D), 1.0, 6.0, ((0, 128),))
    parents = draw_parents(jax.random.fold_in(key_of[17], 71), 0)
    path = draw_path(jax.random.fold_in(key_of[17], 71), 0)
    cache_len = draw_cache_len(jax.random.fold_in(key_of[17], 71), 0)
    page_table = draw_page_table(jax.random.fold_in(key_of[17], 71), 0)
    kv_pool = draw_kv_pool(jax.random.fold_in(key_of[17], 71), 0)
    mig_slot = set_ends(jax.random.randint(key_of[6], (DEVICES,), 0, R_DEV), jax.random.fold_in(key_of[6], 1), 0, R_DEV - 1).astype(jnp.int32)
    mig_dest = draw_mig_dest(jax.random.fold_in(key_of[17], 71), 0)
    attn_gain = jnp.clip(1.0 + 0.15 * jax.random.normal(key_of[8], (D,), jnp.float32), 0.25, 1.75).astype(jnp.bfloat16)
    w_qkv = gaussian(key_of[9], (D, QKVW), D ** -0.5, 0.15625)
    w_out = gaussian(key_of[10], (QUERY_HEADS * HEAD_SIZE, D), (QUERY_HEADS * HEAD_SIZE) ** -0.5, 0.15625)
    moe_gain = jnp.clip(1.0 + 0.15 * jax.random.normal(key_of[11], (D,), jnp.float32), 0.25, 1.75).astype(jnp.bfloat16)
    w_router = gaussian(key_of[12], (D, EXPERTS), D ** -0.5, 0.15625)
    expert_ids_keys = jax.random.split(jax.random.fold_in(key_of[13], 1), TOKENS // TOK_DEV)
    expert_ids_turns = jax.random.permutation(jax.random.fold_in(key_of[13], 3), TOKENS // TOK_DEV)
    expert_ids = jax.vmap(lambda own, number: deal_out(jax.random.fold_in(key_of[13], 2), own, number, TOK_DEV, EXPERTS, TOPK, CAP, 2))(expert_ids_keys, expert_ids_turns).reshape((TOKENS, TOPK))
    w_gate = gaussian(key_of[14], (EXPERTS * SPLIT, D, FFS), D ** -0.5, 0.15625, ((0, 128),))
    w_up = gaussian(key_of[15], (EXPERTS * SPLIT, D, FFS), D ** -0.5, 0.15625, ((0, 128),))
    w_down = gaussian(key_of[16], (EXPERTS * SPLIT, FFS, D), FF ** -0.5, 0.21875, ((0, 128),))
    return dict(hidden=hidden, parents=parents, path=path, cache_len=cache_len, page_table=page_table, kv_pool=kv_pool, mig_slot=mig_slot, mig_dest=mig_dest, attn_gain=attn_gain, w_qkv=w_qkv, w_out=w_out, moe_gain=moe_gain, w_router=w_router, expert_ids=expert_ids, w_gate=w_gate, w_up=w_up, w_down=w_down)


EPSILON = 1e-06
ROPE_BASE = 1000000.0
PRECISE = lax.Precision.HIGHEST
MASKED = -1e+30

def rms_scale(values, scaling):
    widened = values.astype(jnp.float32)
    spread = lax.optimization_barrier(jnp.mean(widened * widened, axis=-1, keepdims=True))
    return (widened * lax.rsqrt(spread + EPSILON) * scaling.astype(jnp.float32)).astype(jnp.bfloat16)

def ancestry(parent_row):
    length = parent_row.shape[-1]
    indices = jnp.arange(length, dtype=jnp.int32)
    linked = (parent_row[:, None] == indices[None, :]).astype(jnp.float32)
    reached = jnp.minimum(linked + jnp.eye(length, dtype=jnp.float32), 1.0)
    for repeat_index in range(max(1, (length - 1).bit_length())):
        reached = jnp.minimum(jnp.dot(reached, reached, precision=PRECISE), 1.0)
    return reached

def apply_rotary(tensor, token_positions):
    halfway = tensor.shape[-1] // 2
    spectrum = ROPE_BASE ** (-2.0 * jnp.arange(halfway, dtype=jnp.float32) / tensor.shape[-1])
    angles = token_positions[..., None] * spectrum
    cosine = jnp.cos(angles)[..., None, :]
    sine_part = jnp.sin(angles)[..., None, :]
    former = tensor[..., :halfway]
    latter = tensor[..., halfway:]
    return jnp.concatenate([former * cosine - latter * sine_part, latter * cosine + former * sine_part], axis=-1)

def take_rows(source_rows, row_ids):
    return source_rows[row_ids]

def reference(hidden, parents, path, cache_len, page_table, kv_pool, mig_slot, mig_dest, attn_gain, w_qkv, w_out, moe_gain, w_router, expert_ids, w_gate, w_up, w_down):
    device_count = N_REQ * N_EP
    device_ids = jnp.arange(device_count, dtype=jnp.int32)
    target = device_ids // N_EP * N_EP + mig_dest
    source = jnp.zeros((device_count,), jnp.int32).at[target].set(device_ids)
    request_ids = jnp.arange(REQUEST_COUNT, dtype=jnp.int32)
    holder = request_ids // R_DEV
    within = request_ids % R_DEV
    sender = source[holder]
    anchor = jnp.where(within == mig_slot[holder], sender * R_DEV + mig_slot[sender], request_ids)
    lengths = cache_len[anchor]
    page_rows = (anchor // R_DEV)[:, None] * POOL + page_table[anchor]
    tree_reach = jax.vmap(ancestry)(parents)
    tree_depth = lax.optimization_barrier(jnp.sum(tree_reach, axis=-1)) - 1.0
    token_positions = lengths.astype(jnp.float32)[:, None] + tree_depth
    query_width = QUERY_HEADS * HEAD_SIZE
    key_width = KEY_VALUE_HEADS * HEAD_SIZE
    normed = rms_scale(hidden, attn_gain)
    projected_input = jnp.dot(normed, w_qkv, preferred_element_type=jnp.float32).reshape(REQUEST_COUNT, DRAFT_TOKENS, QKVW)
    query_rows = apply_rotary(projected_input[..., :query_width].reshape(REQUEST_COUNT, DRAFT_TOKENS, QUERY_HEADS, HEAD_SIZE), token_positions).astype(jnp.bfloat16)
    newest_keys = apply_rotary(projected_input[..., query_width:query_width + key_width].reshape(REQUEST_COUNT, DRAFT_TOKENS, KEY_VALUE_HEADS, HEAD_SIZE), token_positions).astype(jnp.bfloat16)
    newest_values = projected_input[..., query_width + key_width:].astype(jnp.bfloat16)
    fresh_kv = jnp.concatenate([newest_keys.reshape(REQUEST_COUNT, DRAFT_TOKENS, key_width), newest_values], axis=-1)

    def one_request(operands):
        request_query, request_kv, request_pages, cache_length, reached = operands
        cached = kv_pool[request_pages].reshape(CONTEXT_LIMIT, KVW)
        merged_heads = jnp.concatenate([cached, request_kv], axis=0)
        key_head_rows = merged_heads[:, :key_width].reshape(CONTEXT_LIMIT + DRAFT_TOKENS, KEY_VALUE_HEADS, HEAD_SIZE).astype(jnp.float32)
        value_head_rows = merged_heads[:, key_width:].reshape(CONTEXT_LIMIT + DRAFT_TOKENS, KEY_VALUE_HEADS, HEAD_SIZE).astype(jnp.float32)
        grouped_query = request_query.reshape(DRAFT_TOKENS, KEY_VALUE_HEADS, QUERY_HEADS // KEY_VALUE_HEADS, HEAD_SIZE).astype(jnp.float32)
        scores = jnp.einsum('skgd,lkd->kgsl', grouped_query, key_head_rows, precision=PRECISE) * HEAD_SIZE ** (-0.5)
        in_cache = jnp.broadcast_to(jnp.arange(CONTEXT_LIMIT, dtype=jnp.int32)[None, :] < cache_length, (DRAFT_TOKENS, CONTEXT_LIMIT))
        allowed = jnp.concatenate([in_cache, reached > 0.5], axis=1)
        scores = jnp.where(allowed[None, None], scores, MASKED)
        highest = lax.optimization_barrier(jnp.max(scores, axis=-1, keepdims=True))
        weights = jnp.exp(scores - highest)
        totals = lax.optimization_barrier(jnp.sum(weights, axis=-1, keepdims=True))
        mixed = jnp.einsum('kgsl,lkd->kgsd', weights, value_head_rows, precision=PRECISE) / totals
        return jnp.transpose(mixed, (2, 0, 1, 3)).reshape(DRAFT_TOKENS, query_width)
    attended = lax.map(one_request, (query_rows.reshape(REQUEST_COUNT, DRAFT_TOKENS, query_width), fresh_kv, page_rows, lengths, tree_reach)).astype(jnp.bfloat16)
    projected_out = jnp.dot(attended.reshape(TOKENS, query_width), w_out, preferred_element_type=jnp.float32)
    residual_mid = (hidden.astype(jnp.float32) + projected_out).astype(jnp.bfloat16)
    picked_kv = jax.vmap(take_rows)(fresh_kv, jnp.maximum(path, 0))
    compact_kv = jnp.where((path >= 0)[..., None], picked_kv, jnp.zeros((), jnp.bfloat16))
    normed_moe = rms_scale(residual_mid, moe_gain)
    logits = jnp.dot(normed_moe, w_router, preferred_element_type=jnp.float32)
    chosen = jnp.take_along_axis(logits, expert_ids, axis=1)
    squashed = jax.nn.sigmoid(chosen)
    gate_share = squashed / lax.optimization_barrier(jnp.sum(squashed, axis=1, keepdims=True))
    row_limit = N_REQ * N_EP * CAP

    def expert_step(total_moe, expert):
        matches = expert_ids == expert
        chosen_any = jnp.any(matches, axis=1)
        share = lax.optimization_barrier(jnp.sum(jnp.where(matches, gate_share, 0.0), axis=1))
        picked = jnp.nonzero(chosen_any, size=row_limit, fill_value=0)[0]
        valid = jnp.arange(row_limit, dtype=jnp.int32) < jnp.sum(chosen_any.astype(jnp.int32))
        chosen_rows = normed_moe[picked].astype(jnp.float32)
        start = (expert * SPLIT).astype(jnp.int32)
        gate_block = lax.dynamic_slice_in_dim(w_gate, start, SPLIT, 0).astype(jnp.float32)
        up_block = lax.dynamic_slice_in_dim(w_up, start, SPLIT, 0).astype(jnp.float32)
        down_block = lax.dynamic_slice_in_dim(w_down, start, SPLIT, 0).astype(jnp.float32)
        gate_val = jnp.einsum('nd,sdf->nsf', chosen_rows, gate_block, precision=PRECISE)
        up_val = jnp.einsum('nd,sdf->nsf', chosen_rows, up_block, precision=PRECISE)
        activated = (jnp.maximum(gate_val, 0.0) * up_val).astype(jnp.bfloat16)
        pieces = jnp.einsum('nsf,sfd->nsd', activated.astype(jnp.float32), down_block, precision=PRECISE).astype(jnp.bfloat16)
        expert_rows = lax.optimization_barrier(jnp.sum(pieces.astype(jnp.float32), axis=1))
        weighted = jnp.where(valid[:, None], share[picked][:, None] * expert_rows, 0.0)
        return (total_moe.at[picked].add(weighted), None)
    moe_sum, unused_out = lax.scan(expert_step, jnp.zeros((TOKENS, D), jnp.float32), jnp.arange(EXPERTS, dtype=jnp.int32))
    layer_out = (residual_mid.astype(jnp.float32) + moe_sum).astype(jnp.bfloat16)
    return (layer_out, compact_kv)
```

```python
import jax
import jax.numpy as jnp
from jax import lax
from jax.experimental import pallas as pl
from jax.experimental.pallas import tpu as pltpu
from jax.sharding import PartitionSpec as P

QUERY_HEADS = 12
KEY_VALUE_HEADS = 2
HEAD_SIZE = 128
CAP = 32


EPSILON = 1e-06
ROPE_BASE = 1000000.0
PRECISE = lax.Precision.HIGHEST
MASKED = -1e30


def rms_scale(values, scaling):
    widened = values.astype(jnp.float32)
    spread = jnp.mean(widened * widened, axis=-1, keepdims=True)
    return (widened * lax.rsqrt(spread + EPSILON) * scaling.astype(jnp.float32)).astype(
        jnp.bfloat16
    )


def ancestry(parent_row):
    length = parent_row.shape[-1]
    indices = jnp.arange(length, dtype=jnp.int32)
    linked = (parent_row[:, None] == indices[None, :]).astype(jnp.float32)
    reached = jnp.minimum(linked + jnp.eye(length, dtype=jnp.float32), 1.0)
    for repeat_index in range(max(1, (length - 1).bit_length())):
        reached = jnp.minimum(jnp.dot(reached, reached, precision=PRECISE), 1.0)
    return reached


def apply_rotary(tensor, token_positions):
    halfway = tensor.shape[-1] // 2
    spectrum = ROPE_BASE ** (-2.0 * jnp.arange(halfway, dtype=jnp.float32) / tensor.shape[-1])
    angles = token_positions[..., None] * spectrum
    cosine = jnp.cos(angles)[..., None, :]
    sine_part = jnp.sin(angles)[..., None, :]
    former = tensor[..., :halfway]
    latter = tensor[..., halfway:]
    return jnp.concatenate(
        [former * cosine - latter * sine_part, latter * cosine + former * sine_part], axis=-1
    )


def take_rows(source_rows, row_ids):
    return source_rows[row_ids]


def split_into_heads(cache_rows, kv_heads):
    key_width = cache_rows.shape[-1] // 2
    leading = cache_rows.shape[:-1]
    head_shape = leading + (kv_heads, key_width // kv_heads)
    return (
        cache_rows[..., :key_width].reshape(head_shape),
        cache_rows[..., key_width:].reshape(head_shape),
    )


def attend(grouped_query, key_head_rows, value_head_rows, allowed):
    scores = jnp.einsum(
        "skgd,lkd->kgsl", grouped_query, key_head_rows, preferred_element_type=jnp.float32
    ) * grouped_query.shape[-1] ** (-0.5)
    scores = jnp.where(allowed[None, None], scores, MASKED)
    highest = jnp.max(scores, axis=-1)
    weights = jnp.exp(scores - highest[..., None])
    totals = jnp.sum(weights, axis=-1)
    summed = jnp.einsum(
        "kgsl,lkd->kgsd", weights, value_head_rows.astype(jnp.float32), precision=PRECISE
    )
    return (highest, totals, summed)


def blend(first_part, second_part):
    highest = jnp.maximum(first_part[0], second_part[0])
    first_factor = jnp.exp(first_part[0] - highest)
    second_factor = jnp.exp(second_part[0] - highest)
    totals = first_part[1] * first_factor + second_part[1] * second_factor
    summed = first_part[2] * first_factor[..., None] + second_part[2] * second_factor[..., None]
    return summed / totals[..., None]


SLOTS = 1024
ROUNDS = 64
GROUPS = 4
PER_GROUP = ROUNDS // GROUPS
HALF_CAP = CAP // 2
SHARD = 192
MESH = pl.DeviceIdType.MESH


def here():
    req = lax.axis_index("req")
    ep = lax.axis_index("ep")
    return req // 4, req % 4, ep // 2, ep % 2


def partner(place, turn, sign):
    x, z, y, core = place
    dx = (3 * turn) % 4
    dz = (turn + turn // 4) % 4
    other_pair = (turn + turn // 16) % 2
    dcore = (turn // 2 + turn // 32) % 2
    far_x = (x + sign * dx + 4) % 4
    far_z = (z + sign * dz + 4) % 4
    far_y = y * (1 - other_pair) + (3 - y) * other_pair
    return far_x * 4 + far_z, far_y, (core + dcore) % 2


def first_slot(req, y, core):
    return pl.multiple_of((req * 2 + y // 2) * CAP + HALF_CAP * core, HALF_CAP)


def for_each(low, high, act):
    def body(index, carry):
        act(index)
        return carry

    lax.fori_loop(low, high, body, 0)


def experts_kernel(
    normed_ref,
    mid_ref,
    ids_ref,
    router_ref,
    gate_up_ref,
    down_ref,
    out_ref,
    packed,
    arrived,
    results,
    returned,
    gate_up,
    down,
    shares,
    out_sem,
    in_sem,
    back_sem,
    home_sem,
    local_sem,
    weight_send,
    weight_recv,
):
    place = here()
    x, z, y, core = place
    req = lax.axis_index("req")
    mate = (req, y * 2 + 1 - core)
    pair_y = (y // 2) * 2 + 1 - y % 2
    pair = (req, pair_y * 2 + core)

    barrier = pltpu.get_barrier_semaphore()

    def greet(turn):
        far_req, far_y, far_core = partner(place, turn, 1)
        pl.semaphore_signal(
            barrier, inc=1, device_id=(far_req, far_y * 2 + far_core), device_id_type=MESH
        )

    for_each(1, ROUNDS, greet)
    pl.semaphore_signal(barrier, inc=1, device_id=pair, device_id_type=MESH)

    own_gate = pltpu.make_async_copy(gate_up_ref, gate_up.at[:, 0:384], local_sem.at[0])
    own_low = pltpu.make_async_copy(
        down_ref.at[pl.ds(0, 128)], down.at[pl.ds(0, 128)], local_sem.at[1]
    )
    own_high = pltpu.make_async_copy(
        down_ref.at[pl.ds(128, 64)], down.at[pl.ds(256, 64)], local_sem.at[2]
    )
    own_gate.start()
    own_low.start()
    own_high.start()

    tokens = ids_ref.shape[0]
    experts = router_ref.shape[1]
    normed = normed_ref[...]
    logits = jnp.dot(normed, router_ref[...], preferred_element_type=jnp.float32)
    lanes = lax.broadcasted_iota(jnp.int32, (tokens, experts), 1)
    assigned = jnp.zeros((tokens, experts), jnp.float32)
    for choice in range(ids_ref.shape[1]):
        assigned += jnp.where(ids_ref[:, choice : choice + 1] == lanes, 1.0, 0.0)
    earlier = lax.broadcasted_iota(jnp.int32, (tokens, tokens), 0) > lax.broadcasted_iota(
        jnp.int32, (tokens, tokens), 1
    )
    ranks = jnp.dot(
        jnp.where(earlier, 1.0, 0.0).astype(jnp.bfloat16),
        assigned.astype(jnp.bfloat16),
        preferred_element_type=jnp.float32,
    )
    slot_of = jnp.where(assigned > 0.5, ranks, -1.0).astype(jnp.bfloat16)
    squashed = jnp.where(assigned > 0.5, 1.0 / (1.0 + jnp.exp(-logits)), 0.0)
    share = squashed / jnp.sum(squashed, axis=1, keepdims=True)
    share_high = share.astype(jnp.bfloat16)
    share_low = (share - share_high.astype(jnp.float32)).astype(jnp.bfloat16)

    quarter = SLOTS // GROUPS
    slot_rows = lax.broadcasted_iota(jnp.int32, (quarter, experts), 0)
    slot_lanes = lax.broadcasted_iota(jnp.int32, (quarter, experts), 1)
    want = (lax.broadcasted_iota(jnp.int32, (quarter, tokens), 0) % CAP).astype(jnp.float32)
    for part in range(GROUPS):
        spread = jnp.where((slot_rows + part * quarter) // CAP == slot_lanes, 1.0, 0.0)
        named = lax.dot_general(
            spread.astype(jnp.bfloat16),
            slot_of,
            (((1,), (1,)), ((), ())),
            preferred_element_type=jnp.float32,
        )
        table = jnp.where(named == want, 1.0, 0.0).astype(jnp.bfloat16)
        packed[pl.ds(part * quarter, quarter), :] = jnp.dot(
            table, normed, preferred_element_type=jnp.float32
        ).astype(jnp.bfloat16)

    pl.semaphore_wait(barrier, ROUNDS)

    own_gate.wait()
    own_low.wait()
    own_high.wait()
    GATE = [gate_up.at[:, pl.ds(384 * s, 384)] for s in range(4)]
    LOW = [down.at[pl.ds(384 * (s // 2) + 128 * (s % 2), 128)] for s in range(4)]
    HIGH = [down.at[pl.ds(384 * (s // 2) + 256 + 64 * (s % 2), 64)] for s in range(4)]

    def weight_copies(source, target, device, base):
        return [
            pltpu.make_async_remote_copy(
                src_ref=refs[source],
                dst_ref=refs[target],
                send_sem=weight_send.at[base + k],
                recv_sem=weight_recv.at[base + k],
                device_id=device,
                device_id_type=MESH,
            )
            for k, refs in enumerate((GATE, LOW, HIGH))
        ]

    to_pair = weight_copies(0, 2, pair, 0)
    to_mate = weight_copies(0, 1, mate, 3)
    relay = weight_copies(2, 3, mate, 6)

    def outward(turn):
        far_req, far_y, far_core = partner(place, turn, 1)
        return pltpu.make_async_remote_copy(
            src_ref=packed.at[pl.ds(first_slot(far_req, far_y, far_core), HALF_CAP)],
            dst_ref=arrived.at[pl.ds(pl.multiple_of(turn * HALF_CAP, HALF_CAP), HALF_CAP)],
            send_sem=out_sem.at[turn],
            recv_sem=in_sem.at[turn],
            device_id=(far_req, far_y * 2 + far_core),
            device_id_type=MESH,
        )

    def homeward(turn):
        far_req, far_y, far_core = partner(place, turn, -1)
        return pltpu.make_async_remote_copy(
            src_ref=results.at[pl.ds(pl.multiple_of(turn * HALF_CAP, HALF_CAP), HALF_CAP)],
            dst_ref=returned.at[pl.ds(first_slot(req, y, core), HALF_CAP)],
            send_sem=back_sem.at[turn],
            recv_sem=home_sem.at[turn],
            device_id=(far_req, far_y * 2 + far_core),
            device_id_type=MESH,
        )

    for copy in to_pair + to_mate:
        copy.start()
    for_each(1, ROUNDS, lambda turn: outward(turn).start())
    mine = first_slot(req, y, core)
    keep = pltpu.make_async_copy(
        packed.at[pl.ds(mine, HALF_CAP)], arrived.at[pl.ds(0, HALF_CAP)], local_sem.at[0]
    )
    keep.start()

    spread_rows = lax.broadcasted_iota(jnp.int32, (experts, SLOTS), 0)
    spread_lanes = lax.broadcasted_iota(jnp.int32, (experts, SLOTS), 1)
    spread = jnp.where(spread_lanes // CAP == spread_rows, 1.0, 0.0).astype(jnp.bfloat16)
    slot_lane = (lax.broadcasted_iota(jnp.int32, (tokens, SLOTS), 1) % CAP).astype(jnp.float32)
    chosen = jnp.dot(slot_of, spread, preferred_element_type=jnp.float32) == slot_lane
    for half, part in enumerate((share_high, share_low)):
        shares[pl.ds(half * tokens, tokens), :] = jnp.where(
            chosen, jnp.dot(part, spread, preferred_element_type=jnp.float32), 0.0
        ).astype(jnp.bfloat16)

    keep.wait()
    for sent, passed in zip(to_pair, relay):
        sent.wait_recv()
        passed.start()
    for copy in to_mate + relay:
        copy.wait_recv()

    half_lane = lax.broadcasted_iota(jnp.int32, (quarter, 128), 1) < 64
    for group in range(GROUPS):
        low, high = group * PER_GROUP, (group + 1) * PER_GROUP
        for_each(max(low, 1), high, lambda turn: outward(turn).wait_recv())
        rows = arrived[pl.ds(group * quarter, quarter), :]
        hidden = jnp.dot(rows, gate_up[...], preferred_element_type=jnp.float32)
        active = []
        for first in (0, 768):
            blocks = [hidden[:, first + 128 * k : first + 128 * (k + 1)] for k in range(6)]
            active.append(jnp.maximum(blocks[0], 0.0) * blocks[1])
            active.append(jnp.maximum(blocks[3], 0.0) * blocks[4])
            one, two = blocks[2], blocks[5]
            gates = jnp.where(half_lane, one, pltpu.roll(two, 64, 1))
            ups = jnp.where(half_lane, pltpu.roll(one, 64, 1), two)
            active.append(jnp.maximum(gates, 0.0) * ups)
        activated = jnp.concatenate(active, axis=1).astype(jnp.bfloat16)
        results[pl.ds(group * quarter, quarter), :] = jnp.dot(
            activated, down[...], preferred_element_type=jnp.float32
        ).astype(jnp.bfloat16)
        for_each(max(low, 1), high, lambda turn: homeward(turn).start())
        if group == 0:
            keep = pltpu.make_async_copy(
                results.at[pl.ds(0, HALF_CAP)],
                returned.at[pl.ds(mine, HALF_CAP)],
                local_sem.at[1],
            )
            keep.start()

    keep.wait()
    for_each(1, ROUNDS, lambda turn: outward(turn).wait_send())
    for copy in to_pair + to_mate + relay:
        copy.wait_send()
    for_each(1, ROUNDS, lambda turn: homeward(turn).wait())

    gathered = jnp.dot(shares[...], returned[...], preferred_element_type=jnp.float32)
    out_ref[...] = (
        mid_ref[...].astype(jnp.float32) + gathered[:tokens] + gathered[tokens:]
    ).astype(jnp.bfloat16)


def run_experts(normed_moe, residual_mid, expert_ids, w_router, gate_up, down):
    tokens, width = normed_moe.shape
    vmem = pl.BlockSpec(memory_space=pltpu.VMEM)
    return pl.pallas_call(
        experts_kernel,
        out_shape=jax.ShapeDtypeStruct((tokens, width), jnp.bfloat16),
        in_specs=[vmem, vmem, vmem, vmem, pl.BlockSpec(memory_space=pl.ANY), pl.BlockSpec(memory_space=pl.ANY)],
        out_specs=vmem,
        scratch_shapes=[
            pltpu.VMEM((SLOTS, width), jnp.bfloat16),
            pltpu.VMEM((SLOTS, width), jnp.bfloat16),
            pltpu.VMEM((SLOTS, width), jnp.bfloat16),
            pltpu.VMEM((SLOTS, width), jnp.bfloat16),
            pltpu.VMEM((width, 8 * SHARD), jnp.bfloat16),
            pltpu.VMEM((4 * SHARD, width), jnp.bfloat16),
            pltpu.VMEM((2 * tokens, SLOTS), jnp.bfloat16),
            pltpu.SemaphoreType.DMA((ROUNDS,)),
            pltpu.SemaphoreType.DMA((ROUNDS,)),
            pltpu.SemaphoreType.DMA((ROUNDS,)),
            pltpu.SemaphoreType.DMA((ROUNDS,)),
            pltpu.SemaphoreType.DMA((3,)),
            pltpu.SemaphoreType.DMA((9,)),
            pltpu.SemaphoreType.DMA((9,)),
        ],
        compiler_params=pltpu.CompilerParams(
            collective_id=1, has_side_effects=True, vmem_limit_bytes=60 << 20
        ),
    )(normed_moe, residual_mid, expert_ids, w_router, gate_up, down)


def per_device(
    hidden,
    parents,
    path,
    cache_len,
    page_table,
    kv_pool,
    mig_slot,
    mig_dest,
    attn_gain,
    w_qkv,
    w_out,
    moe_gain,
    w_router,
    expert_ids,
    w_gate,
    w_up,
    w_down,
):
    cache_slot_count, draft_length = parents.shape
    req_count = lax.axis_size("req")
    ep_count = lax.axis_size("ep")
    device_count = req_count * ep_count
    query_width = w_out.shape[0]
    kv_width = kv_pool.shape[2]
    key_width = kv_width // 2
    context = page_table.shape[1] * kv_pool.shape[1]
    query_group_width = QUERY_HEADS // KEY_VALUE_HEADS
    model_dim = hidden.shape[1]
    tree_reach = jax.vmap(ancestry)(parents)
    tree_depth = jnp.sum(tree_reach, axis=-1) - 1.0
    leaving_slot = mig_slot[0]
    destination = mig_dest[0]
    ep_ids = jnp.arange(ep_count, dtype=jnp.int32)
    to_dest = ep_ids == destination
    own_cache = kv_pool[page_table].reshape(cache_slot_count, context, kv_width)
    leaving = lax.dynamic_index_in_dim(own_cache, leaving_slot, 0, keepdims=False)
    leave_len = lax.dynamic_index_in_dim(cache_len, leaving_slot, 0, keepdims=False)
    context_ids = jnp.arange(context, dtype=jnp.int32)
    normed = rms_scale(hidden, attn_gain)
    projected_input = jnp.dot(normed, w_qkv, preferred_element_type=jnp.float32).reshape(
        cache_slot_count, draft_length, -1
    )
    outgoing = jnp.where(to_dest[:, None, None], leaving[None], jnp.zeros((), jnp.bfloat16))
    length_out = jnp.where(to_dest, leave_len, 0)
    arrived_pages, arrived_lens = (
        lax.all_to_all(outgoing, "ep", split_axis=0, concat_axis=0, tiled=True),
        lax.all_to_all(length_out, "ep", split_axis=0, concat_axis=0, tiled=True),
    )
    anchor_ep = jnp.sum(jnp.where(arrived_lens > 0, ep_ids, 0))
    lengths = cache_len.at[leaving_slot].set(jnp.sum(arrived_lens))
    paged_caches = own_cache.at[leaving_slot].set(
        lax.dynamic_index_in_dim(arrived_pages, anchor_ep, 0, keepdims=False)
    )
    token_positions = lengths.astype(jnp.float32)[:, None] + tree_depth
    query_rows = apply_rotary(
        projected_input[..., :query_width].reshape(
            cache_slot_count, draft_length, QUERY_HEADS, HEAD_SIZE
        ),
        token_positions,
    ).astype(jnp.bfloat16)
    newest_keys = apply_rotary(
        projected_input[..., query_width : query_width + key_width].reshape(
            cache_slot_count, draft_length, KEY_VALUE_HEADS, HEAD_SIZE
        ),
        token_positions,
    ).astype(jnp.bfloat16)
    newest_values = projected_input[..., query_width + key_width :].astype(jnp.bfloat16)
    query_rows, newest_keys, newest_values = (
        query_rows.reshape(
            cache_slot_count, draft_length, KEY_VALUE_HEADS, query_group_width, HEAD_SIZE
        ),
        newest_keys,
        newest_values.reshape(cache_slot_count, draft_length, KEY_VALUE_HEADS, HEAD_SIZE),
    )
    stored_keys, stored_values = split_into_heads(paged_caches, KEY_VALUE_HEADS)
    cache_part = jax.vmap(attend)(
        query_rows,
        stored_keys,
        stored_values,
        jnp.broadcast_to(
            context_ids[None, None, :] < lengths[:, None, None],
            (cache_slot_count, draft_length, context),
        ),
    )
    draft_part = jax.vmap(attend)(query_rows, newest_keys, newest_values, tree_reach > 0.5)
    mixed = blend(cache_part, draft_part)
    attended = (
        jnp.transpose(mixed, (0, 3, 1, 2, 4))
        .reshape(cache_slot_count * draft_length, query_width)
        .astype(jnp.bfloat16)
    )
    projected_out = jnp.dot(attended, w_out, preferred_element_type=jnp.float32)
    residual_mid = (hidden.astype(jnp.float32) + projected_out).astype(jnp.bfloat16)
    fresh_kv = jnp.concatenate(
        [
            newest_keys.reshape(cache_slot_count, draft_length, key_width),
            newest_values.reshape(cache_slot_count, draft_length, key_width),
        ],
        axis=-1,
    )
    picked_kv = jax.vmap(take_rows)(fresh_kv, jnp.maximum(path, 0))
    compact_kv = jnp.where((path >= 0)[..., None], picked_kv, jnp.zeros((), jnp.bfloat16))
    normed_moe = rms_scale(residual_mid, moe_gain)
    gate_up = jnp.concatenate(
        [w_gate[0, :, :128], w_up[0, :, :128], w_gate[0, :, 128:], w_up[0, :, 128:]], axis=1
    )
    layer_out = run_experts(normed_moe, residual_mid, expert_ids, w_router, gate_up, w_down[0])
    return (layer_out, compact_kv)


def solution(mesh):
    in_specs = (
        P(("req", "ep"), None),
        P(("req", "ep"), None),
        P(("req", "ep"), None),
        P(("req", "ep")),
        P(("req", "ep"), None),
        P(("req", "ep"), None, None),
        P(("req", "ep")),
        P(("req", "ep")),
        P(),
        P(),
        P(),
        P(),
        P(),
        P(("req", "ep"), None),
        P(("req", "ep"), None, None),
        P(("req", "ep"), None, None),
        P(("req", "ep"), None, None),
    )
    out_specs = (P(("req", "ep"), None), P(("req", "ep"), None, None))
    return jax.shard_map(
        per_device, mesh=mesh, in_specs=in_specs, out_specs=out_specs, check_vma=False
    )
```
